512 devices in a mesh: section: 4 (over x), dp: 8 (over z), seq: 16 (over y, core).
Axes of the slice: x: 4, y: 8, z: 8, core: 2. Of those that a mesh axis runs over, the one named last changes fastest.
Arguments:
- incoming: bfloat16 [4, 8, 2048, 4096], P('section', 'dp', 'seq'), may hold values from -6 to 6
- chosen: int32 [4, 8, 256], P('section', 'dp'), may hold values from 0 to 2047, as said below
- norm_gain: float32 [4, 4096], P('section'), may hold values from 0.1 to 1.9
- router: bfloat16 [4, 4096], P('section'), may hold values from -0.25 to 0.25
- w_query: bfloat16 [4, 4096, 4096], P('section', 'dp', 'seq'), may hold values from -1 to 1
- w_key: bfloat16 [4, 4096, 4096], P('section', 'dp', 'seq'), may hold values from -1 to 1
- w_value: bfloat16 [4, 4096, 4096], P('section', 'dp', 'seq'), may hold values from -0.09375 to 0.09375
- w_out_t: bfloat16 [4, 4096, 4096], P('section', 'dp', 'seq'), may hold values from -0.5 to 0.5
Outputs:
- outgoing: bfloat16 [4, 8, 2048, 4096], P('section', 'dp', 'seq')
The draws below stay inside these ranges and needn't reach their ends.
Inputs may be any that keep to these rules, and one draw needn't show every extreme that they name: chosen[s, b] holds 256 distinct positions in increasing order; each aligned block of 128 positions holds at most 32 of them, and in every sequence one block holds exactly 32.
All inputs are finite; a program needn't handle non-finite values.
Results may differ from the reference program's by a relative error of at most 0.014.
Values may be sent and summed in bfloat16 or wider, within the bound.
No kernel may reach another device: no remote copies, remote signals or barrier semaphores. Data moves between devices by JAX's collectives and lax.ppermute only.
A program may use at most 64 MiB of HBM per device.

```python
import jax
import jax.numpy as jnp
from jax import lax

D = 4096
HEADS = 32
HD = 128
TOK_DEV = 128
SECTIONS = 4
BATCH = 8
LEN = 2048
CHOSEN = 256
MOST = 32
N_SEQ = 16


def draw_chosen(key, part):
    shard_count = LEN // TOK_DEV
    row_count = SECTIONS * BATCH
    base_key = jax.random.fold_in(key, 11)
    key_heavy, key_weight, key_score = jax.random.split(base_key, 3)
    heavy_shard = jax.random.randint(key_heavy, (row_count, 1), 0, shard_count)
    shard_ids = jnp.arange(shard_count, dtype=jnp.int32)[None, :]
    is_heavy = shard_ids == heavy_shard
    shares = jax.random.randint(key_weight, (row_count, shard_count), 1, 3)
    shares = jnp.where(is_heavy, 0, shares)
    spare_rows = CHOSEN - MOST
    share_sum = jnp.sum(shares, axis=1, keepdims=True)
    floors = spare_rows * shares // share_sum
    leftover = spare_rows - jnp.sum(floors, axis=1, keepdims=True)
    others = 1 - is_heavy.astype(jnp.int32)
    slot_rank = jnp.cumsum(others, axis=1) - others
    extra_one = jnp.where((others == 1) & (slot_rank < leftover), 1, 0)
    counts = floors + extra_one + jnp.where(is_heavy, MOST, 0)
    scores = jax.random.randint(key_score, (row_count, shard_count, TOK_DEV), 0, 1 << 20) * TOK_DEV + jnp.arange(TOK_DEV, dtype=jnp.int32)
    order_ids = jnp.argsort(scores, axis=-1)
    rank_ids = jnp.argsort(order_ids, axis=-1)
    taken_mask = rank_ids < counts[:, :, None]
    flat_mask = taken_mask.reshape(row_count, LEN)
    sort_key = jnp.where(flat_mask, 0, LEN) + jnp.arange(LEN, dtype=jnp.int32)
    picked = jnp.argsort(sort_key, axis=-1)[:, :CHOSEN]
    return picked.astype(jnp.int32).reshape(SECTIONS, BATCH, CHOSEN)


def draw_w_query(key, part):
    drawn = jax.random.normal(jax.random.fold_in(key, 1), (SECTIONS, D, HEADS * HD), jnp.float32) * D ** (-0.5)
    return jnp.clip(drawn, -1.0, 1.0).astype(jnp.bfloat16)


def draw_w_key(key, part):
    drawn = jax.random.normal(jax.random.fold_in(key, 3), (SECTIONS, D, HEADS * HD), jnp.float32) * D ** (-0.5)
    return jnp.clip(drawn, -1.0, 1.0).astype(jnp.bfloat16)


def block_levels(stream_key, extent, cuts, low, largest):
    level = 1.0
    for dim, shards_of in cuts:
        draws = jax.random.uniform(jax.random.fold_in(jax.random.fold_in(stream_key, 6), dim), (shards_of,), jnp.float32, low / len(cuts), largest / len(cuts))
        level = level * jnp.repeat(jnp.exp(draws), extent[dim] // shards_of).reshape((-1,) + (1,) * (len(extent) - 1 - dim))
    return level


def centred(key, extent, deviation, most, cuts=(), held_as=jnp.bfloat16):
    result = deviation * jax.random.normal(key, extent, jnp.float32)
    if cuts:
        result = result * block_levels(key, extent, cuts, -0.22, 0.18)
    return jnp.clip(result, -most, most).astype(held_as)


def setup_inputs(seed: int = 0) -> dict:
    splits = jax.random.split(jax.random.key(seed), 9)
    incoming = centred(splits[0], (SECTIONS, BATCH, LEN, D), 1.0, 6.0, ((0, 4), (1, 8), (2, 16)))
    chosen = draw_chosen(jax.random.fold_in(splits[8], 71), 0)
    norm_gain = jnp.clip(1.0 + 0.18 * jax.random.normal(splits[2], (SECTIONS, D), jnp.float32), 0.1, 1.9)
    router = centred(splits[3], (SECTIONS, D), (D // 9) ** -0.5, 0.25, ((0, 4),))
    w_query = draw_w_query(jax.random.fold_in(splits[8], 71), 0)
    w_key = draw_w_key(jax.random.fold_in(splits[8], 71), 0)
    w_value = centred(splits[6], (SECTIONS, D, HEADS * HD), D ** -0.5, 0.09375, ((0, 4), (1, 8), (2, 16)))
    w_out_t = centred(splits[7], (SECTIONS, D, HEADS * HD), HD ** -0.5, 0.5, ((0, 4), (1, 8), (2, 16)))
    return {"incoming": incoming, "chosen": chosen, "norm_gain": norm_gain, "router": router, "w_query": w_query, "w_key": w_key, "w_value": w_value, "w_out_t": w_out_t}


EPSILON = 1e-05
ROPE_BASE = 500000.0
NEG_FILL = -1e+30

def rms_norm(rows_in, gain_vec):
    widened = rows_in.astype(jnp.float32)
    inv_scale = lax.rsqrt(lax.optimization_barrier(jnp.mean(widened * widened, axis=-1, keepdims=True)) + EPSILON)
    return (widened * inv_scale * gain_vec[None, :]).astype(jnp.bfloat16)

def apply_rope(projected, positions):
    half_dim = HD // 2
    inverse_freq = ROPE_BASE ** (-2.0 * jnp.arange(half_dim, dtype=jnp.float32) / HD)
    angles = positions.astype(jnp.float32)[:, None] * inverse_freq[None, :]
    cosine = jnp.cos(angles)[:, None, :]
    sine_vals = jnp.sin(angles)[:, None, :]
    shaped = projected.reshape(projected.shape[0], -1, HD)
    first_half = shaped[:, :, :half_dim]
    second_half = shaped[:, :, half_dim:]
    rotated = jnp.concatenate([first_half * cosine - second_half * sine_vals, second_half * cosine + first_half * sine_vals], axis=-1)
    return rotated.reshape(projected.shape)

def attend(queries, keys_in, values_in, query_pos, key_pos):
    heads_split = queries.reshape(queries.shape[0], -1, HD).astype(jnp.float32)
    keys_split = keys_in.reshape(keys_in.shape[0], -1, HD).astype(jnp.float32)
    values_split = values_in.reshape(values_in.shape[0], -1, HD).astype(jnp.float32)
    scores = jnp.einsum('qhd,khd->hqk', heads_split, keys_split) * HD ** (-0.5)
    allowed = key_pos[None, :] <= query_pos[:, None]
    scores = jnp.where(allowed[None, :, :], scores, NEG_FILL)
    peak_val = lax.optimization_barrier(jnp.max(scores, axis=-1, keepdims=True))
    exponent = jnp.exp(scores - peak_val)
    attn_weights = (exponent / lax.optimization_barrier(jnp.sum(exponent, axis=-1, keepdims=True))).astype(jnp.bfloat16)
    mixed = jnp.einsum('hqk,khd->qhd', attn_weights.astype(jnp.float32), values_split)
    return mixed.astype(jnp.bfloat16).reshape(queries.shape)

def mod_block(tokens, pick_list, gain_vec, gate_vec, w_q, w_k, w_v, w_o):
    picked = jnp.take(tokens, pick_list, axis=0)
    gates = jax.nn.sigmoid(jnp.dot(picked, gate_vec, preferred_element_type=jnp.float32))
    normed = rms_norm(picked, gain_vec)
    queries = apply_rope(jnp.dot(normed, w_q, preferred_element_type=jnp.float32), pick_list).astype(jnp.bfloat16)
    keys_rot = apply_rope(jnp.dot(normed, w_k, preferred_element_type=jnp.float32), pick_list).astype(jnp.bfloat16)
    values_out = jnp.dot(normed, w_v, preferred_element_type=jnp.float32).astype(jnp.bfloat16)
    attended = attend(queries, keys_rot, values_out, pick_list, pick_list)
    group_cols = w_o.shape[1] // N_SEQ
    grouped = attended.astype(jnp.float32).reshape(attended.shape[0], N_SEQ, group_cols)
    out_grouped = w_o.astype(jnp.float32).reshape(w_o.shape[0], N_SEQ, group_cols)
    partials = jnp.einsum('cgk,dgk->gcd', grouped, out_grouped).astype(jnp.bfloat16)
    partials = lax.optimization_barrier(partials)
    delta = lax.optimization_barrier(jnp.sum(partials.astype(jnp.float32), axis=0)).astype(jnp.bfloat16)
    updated = (picked.astype(jnp.float32) + gates[:, None] * delta.astype(jnp.float32)).astype(jnp.bfloat16)
    return tokens.at[pick_list].set(updated)

def reference(incoming, chosen, norm_gain, router, w_query, w_key, w_value, w_out_t):
    arrived = jnp.roll(incoming, 1, axis=0)

    def per_section(section_items):
        seq_block, pick_block, gain_vec, gate_vec, w_q, w_k, w_v, w_o = section_items

        def per_seq(seq_items):
            tokens, pick_list = seq_items
            return mod_block(tokens, pick_list, gain_vec, gate_vec, w_q, w_k, w_v, w_o)
        return lax.map(per_seq, (seq_block, pick_block))
    return lax.map(per_section, (arrived, chosen, norm_gain, router, w_query, w_key, w_value, w_out_t))
```

```python
import jax
import jax.numpy as jnp
from jax import lax
from jax.sharding import PartitionSpec as P

HD = 128
EPSILON = 1e-05
ROPE_BASE = 500000.0
NEG_FILL = -1e30
SLOTS = 32


def shifted(value, axis, steps):
    count = lax.axis_size(axis)
    pairs = [(source, (source + steps) % count) for source in range(count)]
    return lax.ppermute(value, axis, pairs)


def swapped(value):
    return lax.ppermute(value, "seq", [(i, i ^ 1) for i in range(lax.axis_size("seq"))])


def core_groups():
    count = lax.axis_size("seq")
    return [list(range(0, count, 2)), list(range(1, count, 2))]


def exchange(value, groups=None):
    return lax.all_to_all(
        value, "seq", split_axis=0, concat_axis=0, axis_index_groups=groups, tiled=True
    )


def two_way_ring(block):
    count = lax.axis_size("dp")
    pieces = [None] * count
    pieces[0] = block
    up = down = block
    for step in range(1, count // 2):
        up = shifted(up, "dp", 1)
        down = shifted(down, "dp", -1)
        pieces[count - step] = up
        pieces[step] = down
    half = block.shape[0] // 2
    pieces[count // 2] = jnp.concatenate(
        [shifted(up[:half], "dp", 1), shifted(down[half:], "dp", -1)], axis=0
    )
    return pieces


def rms_norm(rows_in, gain_vec):
    widened = rows_in.astype(jnp.float32)
    inv_scale = lax.rsqrt(jnp.mean(widened * widened, axis=-1, keepdims=True) + EPSILON)
    return (widened * inv_scale * gain_vec[None, :]).astype(jnp.bfloat16)


def rotate(projected, cosine, sine_vals):
    shaped = projected.reshape(projected.shape[0], -1, HD)
    first_half = shaped[:, :, : HD // 2]
    second_half = shaped[:, :, HD // 2 :]
    rotated = jnp.concatenate(
        [
            first_half * cosine - second_half * sine_vals,
            second_half * cosine + first_half * sine_vals,
        ],
        axis=-1,
    )
    return rotated.astype(jnp.bfloat16)


def attend_rows(joint_proj, positions, head_width):
    inverse_freq = ROPE_BASE ** (-2.0 * jnp.arange(HD // 2, dtype=jnp.float32) / HD)
    angles = positions.astype(jnp.float32)[:, None] * inverse_freq[None, :]
    cosine = jnp.cos(angles)[:, None, :]
    sine_vals = jnp.sin(angles)[:, None, :]
    queries = rotate(joint_proj[:, :head_width], cosine, sine_vals)
    keys_rot = rotate(joint_proj[:, head_width : 2 * head_width], cosine, sine_vals)
    values_out = joint_proj[:, 2 * head_width :].astype(jnp.bfloat16)
    values_split = values_out.reshape(values_out.shape[0], -1, HD)
    scores = jnp.einsum(
        "qhd,khd->hqk", queries, keys_rot, preferred_element_type=jnp.float32
    ) * HD ** (-0.5)
    count = positions.shape[0]
    order = jnp.arange(count, dtype=jnp.int32)
    scores = jnp.where((order[None, :] <= order[:, None])[None], scores, NEG_FILL)
    peak_val = jnp.max(scores, axis=-1, keepdims=True)
    exponent = jnp.exp(scores - peak_val)
    attn_weights = (exponent / jnp.sum(exponent, axis=-1, keepdims=True)).astype(jnp.bfloat16)
    mixed = jnp.einsum(
        "hqk,khd->qhd", attn_weights, values_split, preferred_element_type=jnp.float32
    )
    return mixed.astype(jnp.bfloat16).reshape(count, head_width)


def selection(picks, base, block_rows):
    local = picks - base
    slot = jnp.arange(picks.shape[0], dtype=jnp.int32) - jnp.sum((local < 0).astype(jnp.int32))
    live = (local >= 0) & (local < block_rows)
    slot_ids = jnp.arange(SLOTS, dtype=jnp.int32)
    match = (slot[None, :] == slot_ids[:, None]) & live[None, :]
    row_of = jnp.sum(jnp.where(match, local[None, :] + 1, 0), axis=1) - 1
    return row_of[:, None] == jnp.arange(block_rows, dtype=jnp.int32)[None, :]


def pick_product(one_hot, rows, contract):
    return lax.dot_general(
        one_hot.astype(jnp.bfloat16),
        rows,
        (((contract,), (0,)), ((), ())),
        preferred_element_type=jnp.float32,
    )


def rolled(blocks, start):
    return lax.dynamic_slice_in_dim(
        jnp.concatenate([blocks, blocks], axis=0), start, blocks.shape[0], axis=0
    )


def per_device(incoming, chosen, norm_gain, router, w_query, w_key, w_value, w_out_t):
    shards = lax.axis_size("seq")
    members = lax.axis_size("dp")
    my_index = lax.axis_index("seq")
    my_core = my_index % 2
    my_member = lax.axis_index("dp")
    tok_dev, width = incoming.shape[2:]
    base = my_index * tok_dev
    picks = chosen[0, 0]
    total = picks.shape[0]
    feat = width // shards
    groups = core_groups()

    picks_next = shifted(chosen, "section", -1)[0, 0]
    raw_next = pick_product(
        selection(picks_next, base, tok_dev), incoming[0, 0], 1
    ).astype(jnp.bfloat16)
    raw_rows = shifted(raw_next, "section", 1)
    raw_rows, rest = lax.optimization_barrier((raw_rows, incoming))
    tokens = shifted(rest, "section", 1)[0, 0]

    joint = jnp.concatenate([w_query[0], w_key[0], w_value[0]], axis=1)
    half_rows = joint.shape[0] // 2
    joint = rolled(joint.reshape(2, half_rows, -1), my_core).reshape(joint.shape)
    w_back = w_out_t[0]
    head_cols = w_back.shape[1]
    back_halves = rolled(w_back.reshape(2, half_rows, head_cols), my_core)
    back = jnp.concatenate([back_halves[0], swapped(back_halves[1])], axis=1)
    joint_ring = two_way_ring(joint)
    back_ring = two_way_ring(back)

    block_of = picks // tok_dev
    before = jnp.sum((picks[None, :] < (block_of * tok_dev)[:, None]).astype(jnp.int32), axis=1)
    place = block_of * SLOTS + jnp.arange(total, dtype=jnp.int32) - before
    compact = place[:, None] == jnp.arange(shards * SLOTS, dtype=jnp.int32)[None, :]

    router_gate = jax.nn.sigmoid(jnp.dot(raw_rows, router[0], preferred_element_type=jnp.float32))
    normed = rms_norm(raw_rows, norm_gain[0])
    by_feature = normed.reshape(SLOTS, shards, feat).transpose(1, 0, 2)
    by_feature = rolled(by_feature, 2 * my_member)
    slots_in = exchange(by_feature).reshape(shards * SLOTS, feat)
    rows_feat = pick_product(compact, slots_in, 1).astype(jnp.bfloat16)
    own_half = exchange(
        jnp.broadcast_to(rows_feat[None], (members,) + rows_feat.shape), groups
    )
    other_half = swapped(own_half)

    joint_proj = jnp.zeros((total, joint.shape[1]), jnp.float32)
    for r in range(members):
        x_block = jnp.concatenate([own_half[r], other_half[r]], axis=1)
        joint_proj = joint_proj + jnp.dot(
            x_block, joint_ring[r], preferred_element_type=jnp.float32
        )
    attended = attend_rows(joint_proj, picks, head_cols)
    attended = jnp.concatenate([attended, swapped(attended)], axis=1)
    partials = jnp.stack(
        [
            lax.dot_general(
                attended, piece, (((1,), (1,)), ((), ())), preferred_element_type=jnp.float32
            ).astype(jnp.bfloat16)
            for piece in back_ring
        ]
    )
    delta = jnp.sum(exchange(partials, groups).astype(jnp.float32), axis=0).astype(jnp.bfloat16)
    slots_out = pick_product(compact, delta, 0).astype(jnp.bfloat16)
    slots_out = exchange(slots_out.reshape(shards, SLOTS, feat))
    slots_out = rolled(slots_out, (shards - 2 * my_member) % shards)
    summed = slots_out.transpose(1, 0, 2).reshape(SLOTS, width)
    updated = (
        raw_rows.astype(jnp.float32) + router_gate[:, None] * summed.astype(jnp.float32)
    ).astype(jnp.bfloat16)
    mine = selection(picks, base, tok_dev)
    placed = pick_product(mine, updated, 0).astype(jnp.bfloat16)
    result = jnp.where(jnp.any(mine, axis=0)[:, None], placed, tokens)
    return result[None, None]


def solution(mesh):
    in_specs = (
        P("section", "dp", "seq", None),
        P("section", "dp", None),
        P("section", None),
        P("section", None),
        P("section", "dp", "seq"),
        P("section", "dp", "seq"),
        P("section", "dp", "seq"),
        P("section", "dp", "seq"),
    )
    out_specs = P("section", "dp", "seq", None)
    return jax.shard_map(
        per_device, mesh=mesh, in_specs=in_specs, out_specs=out_specs, check_vma=False
    )
```
